32 devices in a mesh: fiber: 16 (over z, y, x), wave: 2 (over core).
Axes of the slice: x: 2, y: 2, z: 4, core: 2. Of those that a mesh axis runs over, the one named last changes fastest.
Arguments:
- spectra: float32 [4, 640, 8192], P(None, 'fiber', 'wave'), may hold values from 0 to 10
- inverse_var: float32 [4, 640, 8192], P(None, 'fiber', 'wave'), may hold values from 0.1 to 10
- mask_bits: int32 [4, 640, 8192], P(None, 'fiber', 'wave'), may hold values from 0 to 512, as said below
- sky_flags: int32 [4, 640], P(None, 'fiber'), may hold values 0 or 1
- fiber_ids: int32 [640], P('fiber'), may hold values from 0 to 639, each once
- positions: float32 [2, 640], replicated, may hold values from -1 to 1
- throughput: float32 [4, 640], P(None, 'fiber'), may hold values from 0.5 to 1.5
Outputs:
- residual: float32 [4, 640, 8192], P(None, 'fiber', 'wave')
- chi_square: float32 [4, 640], P(None, 'fiber')
- sky_coeffs: float32 [16, 8192], P(None, 'wave')
The draws below stay inside these ranges and needn't reach their ends.
Inputs may be any that keep to these rules, and one draw needn't show every extreme that they name: `mask_bits`: each entry is zero or one single bit of 0 to 9. `fiber_ids`: each fiber id appears in exactly one slot.
All inputs are finite; a program needn't handle non-finite values. No bound on the sum of `sky_flags` on one device may be relied on, other than what follows from the above.
Results may differ from the reference program's by a relative error of at most 0.0003.
Values sent between devices are 32-bit elements; how exact they have to be, the bound alone decides.
A program may use at most 64 MiB of HBM per device.

```python
import math
import jax
import jax.numpy as jnp
from jax import lax

E = 4
PARAMS = 16
FIBERS = 640
WAVES = 8192


def draw_mask_bits(key, part):
    raw = jax.random.randint(key, (E, FIBERS, WAVES), 0, 64)
    flagged = jnp.left_shift(jnp.ones_like(raw), raw % 10)
    return jnp.where(raw < 20, flagged, 0).astype(jnp.int32)


def set_ends(drawn, key, smallest, high):
    index_at = [jax.random.randint(jax.random.fold_in(key, axis), (), 0, length) for axis, length in enumerate(drawn.shape)]
    main_axis = drawn.shape.index(max(drawn.shape))
    beside = index_at[:main_axis] + [(index_at[main_axis] + 1) % drawn.shape[main_axis]] + index_at[main_axis + 1:]
    return drawn.at[tuple(index_at)].set(smallest).at[tuple(beside)].set(high)


def shard_levels(rng, dims, pieces, least, top_value):
    factor_of = 1.0
    for dim, shards_of in pieces:
        heights = jax.random.uniform(jax.random.fold_in(jax.random.fold_in(rng, 6), dim), (shards_of,), jnp.float32, least / len(pieces), top_value / len(pieces))
        factor_of = factor_of * jnp.repeat(jnp.exp(heights), dims[dim] // shards_of).reshape((-1,) + (1,) * (len(dims) - 1 - dim))
    return factor_of


def setup_inputs(seed: int = 0) -> dict:
    key_list = jax.random.split(jax.random.key(seed), 8)
    return {
        "spectra": jnp.clip(10.0 * jax.random.uniform(key_list[0], (E, FIBERS, WAVES), jnp.float32) ** shard_levels(key_list[0], (E, FIBERS, WAVES), ((1, 16), (2, 2)), -0.2, 0.2), 0.0, 10.0),
        "inverse_var": jnp.clip(jnp.exp(math.log(10.0) - 4.6051702 * jax.random.uniform(key_list[1], (E, FIBERS, WAVES), jnp.float32) ** shard_levels(key_list[1], (E, FIBERS, WAVES), ((1, 16), (2, 2)), -0.2, 0.2)), 0.1, 10.0),
        "mask_bits": draw_mask_bits(jax.random.fold_in(key_list[7], 71), 0),
        "sky_flags": set_ends((jax.random.randint(key_list[3], (E, FIBERS), 0, 8) < 1).astype(jnp.int32), jax.random.fold_in(key_list[3], 1), 0, 1),
        "fiber_ids": jax.random.permutation(key_list[4], FIBERS).astype(jnp.int32),
        "positions": jnp.clip(jax.random.uniform(key_list[5], (2, FIBERS), jnp.float32, -1.0, 1.0), -1.0, 1.0),
        "throughput": jnp.clip(1.0 + 0.1 * jax.random.normal(key_list[6], (E, FIBERS), jnp.float32), 0.5, 1.5),
    }


bad_bits = 31
prior_weight = 1.0
highest = lax.Precision.HIGHEST

def legendre(coord):
    return [jnp.ones_like(coord), coord, 1.5 * coord * coord - 0.5, (2.5 * coord * coord - 1.5) * coord]

def build_design(positions, fiber_ids, throughput):
    coord_x = positions[0][fiber_ids]
    coord_y = positions[1][fiber_ids]
    poly_x = legendre(coord_x)
    poly_y = legendre(coord_y)
    basis = jnp.stack([along_x * along_y for along_x in poly_x for along_y in poly_y], axis=-1)
    return throughput[:, :, None] * basis[None]

def solve_normal(matrix, right_side):
    param_count = right_side.shape[0]
    factor = {}
    for column in range(param_count):
        pivot_sum = matrix[column * param_count + column] + prior_weight
        for inner_k in range(column):
            pivot_sum = pivot_sum - factor[column, inner_k] * factor[column, inner_k]
        root_value = jnp.sqrt(pivot_sum)
        factor[column, column] = root_value
        for target in range(column + 1, param_count):
            running = matrix[target * param_count + column]
            for inner_k in range(column):
                running = running - factor[target, inner_k] * factor[column, inner_k]
            factor[target, column] = running / root_value
    interim = []
    for target in range(param_count):
        running = right_side[target]
        for inner_k in range(target):
            running = running - factor[target, inner_k] * interim[inner_k]
        interim.append(running / factor[target, target])
    solved = [None] * param_count
    for target in reversed(range(param_count)):
        running = interim[target]
        for inner_k in range(target + 1, param_count):
            running = running - factor[inner_k, target] * solved[inner_k]
        solved[target] = running / factor[target, target]
    return jnp.stack(solved)

def reference(spectra, inverse_var, mask_bits, sky_flags, fiber_ids, positions, throughput):
    row_count = E * FIBERS
    design = build_design(positions, fiber_ids, throughput).reshape(row_count, PARAMS)
    products = (design[:, :, None] * design[:, None, :]).reshape(row_count, PARAMS * PARAMS)
    sky_rows = sky_flags.reshape(row_count).astype(jnp.float32)
    block_width = 512 if WAVES % 512 == 0 else 128

    def step_fn(index, carry):
        residual_all, coeff_all, chi_sum = carry
        offset = (index * block_width).astype(jnp.int32)
        flux_block = lax.dynamic_slice_in_dim(spectra, offset, block_width, 2).reshape(row_count, block_width)
        ivar_block = lax.dynamic_slice_in_dim(inverse_var, offset, block_width, 2).reshape(row_count, block_width)
        bits_block = lax.dynamic_slice_in_dim(mask_bits, offset, block_width, 2).reshape(row_count, block_width)
        usable = (bits_block & bad_bits == 0).astype(jnp.float32)
        noise_weight = ivar_block * usable
        fit_weights = noise_weight * sky_rows[:, None]
        normal = jnp.dot(products.T, fit_weights, precision=highest)
        right_side = jnp.dot(design.T, fit_weights * flux_block, precision=highest)
        block_coeffs = solve_normal(normal, right_side)
        residual = flux_block - jnp.dot(design, block_coeffs, precision=highest)
        chi_sum = chi_sum + lax.optimization_barrier(jnp.sum(noise_weight * residual * residual, axis=1))
        residual_all = lax.dynamic_update_slice_in_dim(residual_all, residual.reshape(E, FIBERS, block_width), offset, 2)
        coeff_all = lax.dynamic_update_slice_in_dim(coeff_all, block_coeffs, offset, 1)
        return (residual_all, coeff_all, chi_sum)
    start_state = (jnp.zeros((E, FIBERS, WAVES), jnp.float32), jnp.zeros((PARAMS, WAVES), jnp.float32), jnp.zeros((row_count,), jnp.float32))
    residual_all, coeff_all, chi_sum = lax.fori_loop(0, WAVES // block_width, step_fn, start_state)
    chi_square = (chi_sum / WAVES).reshape(E, FIBERS)
    return (residual_all, chi_square, coeff_all)
```

```python
import functools

import jax
import jax.numpy as jnp
from jax import lax
from jax.experimental import pallas as pl
from jax.experimental.pallas import tpu as pltpu
from jax.sharding import PartitionSpec as P

PARAMS = 16

bad_bits = 31
prior_weight = 1.0
highest = lax.Precision.HIGHEST
moment_degrees = 7
basis_degrees = 4
padded_degrees = 8
moment_rows = moment_degrees * padded_degrees
all_rows = moment_rows + PARAMS
lanes = 128
low_size = 4
MESH = pl.DeviceIdType.MESH


def monomial_table(degree_total):
    coeffs = [[0.0] * degree_total for order in range(degree_total)]
    coeffs[0][0] = 1.0
    coeffs[1][1] = 1.0
    for order in range(1, degree_total - 1):
        for power in range(degree_total):
            raised = coeffs[order][power - 1] if power >= 1 else 0.0
            coeffs[order + 1][power] = (
                (2 * order + 1) * raised - order * coeffs[order - 1][power]
            ) / (order + 1)
    return coeffs


def product_series(higher, first, second):
    product = [0.0] * moment_degrees
    for left_power in range(moment_degrees):
        for right_power in range(moment_degrees - left_power):
            product[left_power + right_power] += (
                higher[first][left_power] * higher[second][right_power]
            )
    series = [0.0] * moment_degrees
    for order in reversed(range(moment_degrees)):
        weight_now = product[order] / higher[order][order]
        series[order] = weight_now
        for power in range(moment_degrees):
            product[power] -= weight_now * higher[order][power]
    return series


def rebuild_table(row_degrees):
    higher = monomial_table(moment_degrees)
    pair = [
        [product_series(higher, first, second) for second in range(basis_degrees)]
        for first in range(basis_degrees)
    ]
    degrees = range(basis_degrees)
    return jnp.asarray(
        [
            [
                pair[i][k][a] * pair[j][l][b] if b < moment_degrees else 0.0
                for a in range(moment_degrees)
                for b in range(row_degrees)
            ]
            for i in degrees
            for j in degrees
            for k in degrees
            for l in degrees
        ],
        jnp.float32,
    )


def legendre(coord):
    return [
        jnp.ones_like(coord),
        coord,
        1.5 * coord * coord - 0.5,
        (2.5 * coord * coord - 1.5) * coord,
    ]


def legendre_series(coord, degree_total):
    series = [jnp.ones_like(coord), coord]
    for order in range(1, degree_total - 1):
        series.append(
            ((2 * order + 1) * coord * series[order] - order * series[order - 1]) / (order + 1)
        )
    return series


def exact_dot(left, right):
    return jnp.dot(left, right, precision=highest, preferred_element_type=jnp.float32)


def transposed_dot(left, right):
    return lax.dot_general(
        left, right, (((1,), (1,)), ((), ())), precision=highest, preferred_element_type=jnp.float32
    )


def split_bf16(value):
    high = value.astype(jnp.bfloat16)
    low = (value - high.astype(jnp.float32)).astype(jnp.bfloat16)
    return high, low


def iota(shape, axis):
    return lax.broadcasted_iota(jnp.int32, shape, axis)


def build_features(ids_ref, positions_ref, throughput_ref, flags_ref):
    exposures, fibers = throughput_ref.shape
    rows = exposures * fibers
    total = positions_ref.shape[1]
    pick = (iota((total, fibers), 0) == ids_ref[...]).astype(jnp.float32)
    coords = exact_dot(positions_ref[...], pick)
    column = iota((fibers, rows), 1)
    spread = functools.reduce(
        jnp.logical_or,
        [iota((fibers, rows), 0) + e * fibers == column for e in range(exposures)],
    ).astype(jnp.float32)
    at = iota((exposures, rows), 1) - iota((exposures, rows), 0) * fibers
    own = (at >= 0) & (at < fibers)

    def widen(value):
        return jnp.sum(jnp.where(own, exact_dot(value, spread), 0.0), axis=0, keepdims=True)

    coords = exact_dot(coords, spread)
    coord_x, coord_y = coords[0:1], coords[1:2]
    through = widen(throughput_ref[...])
    flags = widen(flags_ref[...].astype(jnp.float32))
    series_x = legendre_series(coord_x, moment_degrees)
    series_y = legendre_series(coord_y, moment_degrees)
    sub = iota((padded_degrees, rows), 0)
    stack_y = jnp.zeros((padded_degrees, rows), jnp.float32)
    for order in range(moment_degrees):
        stack_y = jnp.where(sub == order, series_y[order], stack_y)
    scale = through * through * flags
    moments = jnp.concatenate([stack_y * (one * scale) for one in series_x], axis=0)
    poly_x, poly_y = legendre(coord_x), legendre(coord_y)
    sub = iota((PARAMS, rows), 0)
    design = jnp.zeros((PARAMS, rows), jnp.float32)
    for k in range(PARAMS):
        value = poly_x[k // basis_degrees] * poly_y[k % basis_degrees]
        design = jnp.where(sub == k, value * through, design)
    return moments, design * flags, design


def solve_block(table, summed):
    width = summed.shape[1]
    normal = exact_dot(table, summed[:moment_rows])
    right = summed[moment_rows:]
    sub = iota((PARAMS, width), 0)
    cols = [
        normal[k * PARAMS:(k + 1) * PARAMS] + jnp.where(sub == k, prior_weight, 0.0)
        for k in range(PARAMS)
    ]
    factor, inverse, interim = [], [], []
    for k in range(PARAMS):
        pivot = cols[k][k:k + 1]
        root = lax.rsqrt(pivot)
        root = root * (1.5 - 0.5 * pivot * root * root)
        inverse.append(root)
        line = cols[k] * root
        factor.append(line)
        value = right[k:k + 1] * root
        interim.append(value)
        right = right - line * value
        for j in range(k + 1, PARAMS):
            cols[j] = cols[j] - line * line[j:j + 1]
    solved = jnp.zeros((PARAMS, width), jnp.float32)
    for k in reversed(range(PARAMS)):
        known = jnp.sum(jnp.where(sub > k, factor[k] * solved, 0.0), axis=0, keepdims=True)
        solved = jnp.where(sub == k, (interim[k] - known) * inverse[k], solved)
    return solved


def kernel(
    fiber_size, wave_size, slices,
    ids_ref, positions_ref, throughput_ref, flags_ref, table_ref,
    spectra_hbm, ivar_hbm, bits_hbm,
    residual_hbm, chi_ref, coeffs_ref,
    flux, noise, bits, resid, moments, gather1, partial, gather2, coeffs,
    chi_mine, chi_other,
    load_sem, store_sem, send_sem, recv_sem, chi_sem,
):
    exposures, fibers, waves = flux.shape
    rows = exposures * fibers
    high_size = fiber_size // low_size
    block = waves // (slices * fiber_size)
    chunk = high_size * block
    me = lax.axis_index("fiber")
    wave_me = lax.axis_index("wave")
    low, high = lax.rem(me, low_size), me // low_size
    low_peer = [high * low_size + lax.rem(low + d, low_size) for d in range(low_size)]
    high_peer = [lax.rem(high + d, high_size) * low_size + low for d in range(high_size)]

    barrier = pltpu.get_barrier_semaphore()
    for peer in low_peer[1:] + high_peer[1:]:
        pl.semaphore_signal(barrier, inc=1, device_id={"fiber": peer}, device_id_type=MESH)
    pl.semaphore_signal(barrier, inc=1, device_id={"wave": 1 - wave_me}, device_id_type=MESH)

    order = [(s, d) for s in range(slices) for d in list(range(1, low_size)) + [0]]

    def span(s, d):
        group = lax.rem(low + d, low_size)
        return group, pl.ds(pl.multiple_of(s * low_size * chunk + group * chunk, chunk), chunk)

    loads = []
    for at, (s, d) in enumerate(order):
        where = span(s, d)[1]
        copies = []
        for n, (source, target) in enumerate(
            ((spectra_hbm, flux), (ivar_hbm, noise), (bits_hbm, bits))
        ):
            copy = pltpu.make_async_copy(
                source.at[:, :, where], target.at[:, :, where], load_sem.at[at, n]
            )
            copy.start()
            copies.append(copy)
        loads.append(copies)

    feature, right_feature, design = build_features(
        ids_ref, positions_ref, throughput_ref, flags_ref
    )
    eye = (iota((rows, rows), 0) == iota((rows, rows), 1)).astype(jnp.float32)
    design_high, design_low = split_bf16(transposed_dot(eye, design))
    design_wide = jnp.concatenate([design_high, design_low, design_high], axis=1)

    pl.semaphore_wait(barrier, low_size - 1 + high_size - 1 + 1)

    def remote(stage, s, d, source, target, peer):
        return pltpu.make_async_remote_copy(
            src_ref=source, dst_ref=target,
            send_sem=send_sem.at[s, stage, d - 1], recv_sem=recv_sem.at[s, stage, d - 1],
            device_id={"fiber": peer}, device_id_type=MESH,
        )

    started = []
    first = {}
    for at, (s, d) in enumerate(order):
        group, where = span(s, d)
        for copy in loads[at]:
            copy.wait()
        good = (bits[:, :, where] & bad_bits) == 0
        weight = jnp.where(good, noise[:, :, where], 0.0)
        noise[:, :, where] = weight
        scaled = (weight * flux[:, :, where]).reshape(rows, chunk)
        normal = exact_dot(feature, weight.reshape(rows, chunk))
        right = exact_dot(right_feature, scaled)
        for b in range(high_size):
            lane = slice(b * block, (b + 1) * block)
            moments[s, group, b, :moment_rows] = normal[:, lane]
            moments[s, group, b, moment_rows:] = right[:, lane]
        if d:
            copy = remote(0, s, d, moments.at[s, group], gather1.at[s, d - 1], low_peer[d])
            copy.start()
            started.append(copy)
            first[s, d] = copy

    def reduce_low(s):
        for d in range(1, low_size):
            first[s, d].wait_recv()
        copies = []
        for d in list(range(1, high_size)) + [0]:
            to = lax.rem(high + d, high_size)
            total = moments[s, low, to]
            for e in range(low_size - 1):
                total = total + gather1[s, e, to]
            partial[s, to] = total
            if d:
                copy = remote(1, s, d, partial.at[s, to], gather2.at[s, d - 1], high_peer[d])
                copy.start()
                copies.append(copy)
        started.extend(copies)
        return copies

    def reduce_high(s, copies):
        for copy in copies:
            copy.wait_recv()
        total = partial[s, high]
        for e in range(high_size - 1):
            total = total + gather2[s, e]
        solved = solve_block(table_ref[...], total)
        mine = coeffs.at[s, low * high_size + high]
        mine[...] = solved
        copies = []
        for d in range(1, high_size):
            copy = remote(2, s, d, mine, mine, high_peer[d])
            copy.start()
            copies.append(copy)
        started.extend(copies)
        return copies

    def spread_low(s, copies):
        for copy in copies:
            copy.wait_recv()
        mine = coeffs.at[s, pl.ds(low * high_size, high_size)]
        copies = []
        for d in range(1, low_size):
            copy = remote(3, s, d, mine, mine, low_peer[d])
            copy.start()
            copies.append(copy)
        started.extend(copies)
        return copies

    stores = []
    chi_total = [jnp.zeros((rows, lanes), jnp.float32)]

    def finish(s, copies):
        for copy in copies:
            copy.wait_recv()
        for group in range(low_size):
            start = (s * low_size + group) * chunk
            where = pl.ds(start, chunk)
            values = jnp.concatenate(
                [coeffs[s, group * high_size + b] for b in range(high_size)], axis=1
            )
            coeffs_ref[:, where] = values
            value_high, value_low = split_bf16(values)
            model = jnp.dot(
                design_wide,
                jnp.concatenate([value_high, value_high, value_low], axis=0),
                preferred_element_type=jnp.float32,
            )
            left = flux[:, :, where].reshape(rows, chunk) - model
            resid[:, :, where] = left.reshape(exposures, fibers, chunk)
            term = noise[:, :, where].reshape(rows, chunk) * left * left
            for n in range(chunk // lanes):
                chi_total[0] = chi_total[0] + term[:, n * lanes:(n + 1) * lanes]
            copy = pltpu.make_async_copy(
                resid.at[:, :, where], residual_hbm.at[:, :, where],
                store_sem.at[s * low_size + group],
            )
            copy.start()
            stores.append(copy)

    stage = {}
    stage[0] = reduce_high(0, reduce_low(0))
    for s in range(1, slices):
        following = reduce_low(s)
        stage[s - 1] = spread_low(s - 1, stage[s - 1])
        stage[s] = reduce_high(s, following)
        finish(s - 1, stage[s - 1])
    finish(slices - 1, spread_low(slices - 1, stage[slices - 1]))

    chi_mine[...] = jnp.zeros_like(chi_mine)
    ones = jnp.ones((8, lanes), jnp.float32)
    for e in range(exposures):
        line = transposed_dot(ones, chi_total[0][e * fibers:(e + 1) * fibers])
        chi_mine[e:e + 1, :fibers] = line[0:1]
    copy = pltpu.make_async_remote_copy(
        src_ref=chi_mine, dst_ref=chi_other, send_sem=chi_sem.at[0], recv_sem=chi_sem.at[1],
        device_id={"wave": 1 - wave_me}, device_id_type=MESH,
    )
    copy.start()
    copy.wait()
    both = chi_mine[:exposures, :fibers] + chi_other[:exposures, :fibers]
    chi_ref[...] = both / (waves * wave_size)
    for copy in stores:
        copy.wait()
    for copy in started:
        copy.wait_send()


def fused_body(fiber_size, wave_size, slices, spectra, inverse_var, mask_bits, sky_flags,
               fiber_ids, positions, throughput):
    exposures, fibers, waves = spectra.shape
    high_size = fiber_size // low_size
    block = waves // (slices * fiber_size)
    table = rebuild_table(padded_degrees)
    vmem = pl.BlockSpec(memory_space=pltpu.VMEM)
    anywhere = pl.BlockSpec(memory_space=pl.ANY)
    cube = (exposures, fibers, waves)
    residual, chi, coeffs = pl.pallas_call(
        functools.partial(kernel, fiber_size, wave_size, slices),
        out_shape=(
            jax.ShapeDtypeStruct(cube, jnp.float32),
            jax.ShapeDtypeStruct((exposures, fibers), jnp.float32),
            jax.ShapeDtypeStruct((PARAMS, waves), jnp.float32),
        ),
        in_specs=[vmem] * 5 + [anywhere] * 3,
        out_specs=(anywhere, vmem, vmem),
        scratch_shapes=[
            pltpu.VMEM(cube, jnp.float32),
            pltpu.VMEM(cube, jnp.float32),
            pltpu.VMEM(cube, jnp.int32),
            pltpu.VMEM(cube, jnp.float32),
            pltpu.VMEM((slices, low_size, high_size, all_rows, block), jnp.float32),
            pltpu.VMEM((slices, low_size - 1, high_size, all_rows, block), jnp.float32),
            pltpu.VMEM((slices, high_size, all_rows, block), jnp.float32),
            pltpu.VMEM((slices, high_size - 1, all_rows, block), jnp.float32),
            pltpu.VMEM((slices, fiber_size, PARAMS, block), jnp.float32),
            pltpu.VMEM((8, lanes), jnp.float32),
            pltpu.VMEM((8, lanes), jnp.float32),
            pltpu.SemaphoreType.DMA((slices * low_size, 3)),
            pltpu.SemaphoreType.DMA((slices * low_size,)),
            pltpu.SemaphoreType.DMA((slices, 4, max(low_size, high_size) - 1)),
            pltpu.SemaphoreType.DMA((slices, 4, max(low_size, high_size) - 1)),
            pltpu.SemaphoreType.DMA((2,)),
        ],
        compiler_params=pltpu.CompilerParams(
            collective_id=0, has_side_effects=True, vmem_limit_bytes=40 * 1024 * 1024
        ),
    )(fiber_ids.reshape(1, fibers), positions, throughput, sky_flags, table,
      spectra, inverse_var, mask_bits)
    return residual, chi, coeffs


def solve_normal(matrix, right_side):
    param_count = right_side.shape[0]
    factor = {}
    for column in range(param_count):
        pivot_sum = matrix[column * param_count + column] + prior_weight
        for inner_k in range(column):
            pivot_sum = pivot_sum - factor[column, inner_k] * factor[column, inner_k]
        root_value = jnp.sqrt(pivot_sum)
        factor[column, column] = root_value
        for target in range(column + 1, param_count):
            running = matrix[target * param_count + column]
            for inner_k in range(column):
                running = running - factor[target, inner_k] * factor[column, inner_k]
            factor[target, column] = running / root_value
    interim = []
    for target in range(param_count):
        running = right_side[target]
        for inner_k in range(target):
            running = running - factor[target, inner_k] * interim[inner_k]
        interim.append(running / factor[target, target])
    solved = [None] * param_count
    for target in reversed(range(param_count)):
        running = interim[target]
        for inner_k in range(target + 1, param_count):
            running = running - factor[inner_k, target] * solved[inner_k]
        solved[target] = running / factor[target, target]
    return jnp.stack(solved)


def plain_body(spectra, inverse_var, mask_bits, sky_flags, fiber_ids, positions, throughput):
    exposures, fiber_count, wave_count = spectra.shape
    row_count = exposures * fiber_count
    coord_x = positions[0][fiber_ids]
    coord_y = positions[1][fiber_ids]

    def stack(first, second, scale):
        basis = jnp.stack([x * y for x in first for y in second], axis=-1)
        return (scale[:, :, None] * basis[None]).reshape(row_count, -1)

    design = stack(legendre(coord_x), legendre(coord_y), throughput)
    products = stack(
        legendre_series(coord_x, moment_degrees),
        legendre_series(coord_y, moment_degrees),
        throughput * throughput,
    )
    flux_rows = spectra.reshape(row_count, wave_count)
    usable = (mask_bits.reshape(row_count, wave_count) & bad_bits == 0).astype(jnp.float32)
    noise_weight = inverse_var.reshape(row_count, wave_count) * usable
    fit_weights = noise_weight * sky_flags.reshape(row_count).astype(jnp.float32)[:, None]
    normal = jnp.dot(products.T, fit_weights, precision=highest)
    right_side = jnp.dot(design.T, fit_weights * flux_rows, precision=highest)
    normal, right_side = lax.psum((normal, right_side), "fiber")
    normal = jnp.dot(rebuild_table(moment_degrees), normal, precision=highest)
    sky_coeffs = solve_normal(normal, right_side)
    residual = flux_rows - jnp.dot(design, sky_coeffs, precision=highest)
    chi_local = jnp.sum(noise_weight * residual * residual, axis=1)
    chi_total = lax.psum(chi_local, "wave")
    chi_square = (chi_total / (wave_count * lax.axis_size("wave"))).reshape(exposures, fiber_count)
    return (residual.reshape(exposures, fiber_count, wave_count), chi_square, sky_coeffs)


def choose_body(fiber_size, wave_size, spectra, *rest):
    exposures, fibers, waves = spectra.shape
    whole = fiber_size % low_size == 0 and fiber_size > low_size and wave_size == 2
    if whole and fibers % 8 == 0 and fibers <= lanes and exposures <= 8:
        for slices in (2, 1):
            if waves % (slices * fiber_size * lanes) == 0:
                return fused_body(fiber_size, wave_size, slices, spectra, *rest)
    return plain_body(spectra, *rest)


def solution(mesh):
    placed = (
        P(None, "fiber", "wave"),
        P(None, "fiber", "wave"),
        P(None, "fiber", "wave"),
        P(None, "fiber"),
        P("fiber"),
        P(),
        P(None, "fiber"),
    )
    return jax.shard_map(
        functools.partial(choose_body, mesh.shape["fiber"], mesh.shape["wave"]),
        mesh=mesh,
        in_specs=placed,
        out_specs=(P(None, "fiber", "wave"), P(None, "fiber"), P(None, "wave")),
        check_vma=False,
    )
```

```python
import functools

import jax
import jax.numpy as jnp
from jax import lax
from jax.experimental import pallas as pl
from jax.experimental.pallas import tpu as pltpu
from jax.sharding import PartitionSpec as P

PARAMS = 16

bad_bits = 31
prior_weight = 1.0
highest = lax.Precision.HIGHEST
moment_degrees = 7
basis_degrees = 4
padded_degrees = 8
moment_rows = moment_degrees * padded_degrees
lanes = 128
low_size = 4
MESH = pl.DeviceIdType.MESH


def monomial_table(degree_total):
    coeffs = [[0.0] * degree_total for order in range(degree_total)]
    coeffs[0][0] = 1.0
    coeffs[1][1] = 1.0
    for order in range(1, degree_total - 1):
        for power in range(degree_total):
            raised = coeffs[order][power - 1] if power >= 1 else 0.0
            coeffs[order + 1][power] = (
                (2 * order + 1) * raised - order * coeffs[order - 1][power]
            ) / (order + 1)
    return coeffs


def product_series(higher, first, second):
    product = [0.0] * moment_degrees
    for left_power in range(moment_degrees):
        for right_power in range(moment_degrees - left_power):
            product[left_power + right_power] += (
                higher[first][left_power] * higher[second][right_power]
            )
    series = [0.0] * moment_degrees
    for order in reversed(range(moment_degrees)):
        weight_now = product[order] / higher[order][order]
        series[order] = weight_now
        for power in range(moment_degrees):
            product[power] -= weight_now * higher[order][power]
    return series


def rebuild_table(row_degrees):
    higher = monomial_table(moment_degrees)
    pair = [
        [product_series(higher, first, second) for second in range(basis_degrees)]
        for first in range(basis_degrees)
    ]
    degrees = range(basis_degrees)
    return jnp.asarray(
        [
            [
                pair[i][k][a] * pair[j][l][b] if b < moment_degrees else 0.0
                for a in range(moment_degrees)
                for b in range(row_degrees)
            ]
            for i in degrees
            for j in degrees
            for k in degrees
            for l in degrees
        ],
        jnp.float32,
    )


def legendre(coord):
    return [
        jnp.ones_like(coord),
        coord,
        1.5 * coord * coord - 0.5,
        (2.5 * coord * coord - 1.5) * coord,
    ]


def legendre_series(coord, degree_total):
    series = [jnp.ones_like(coord), coord]
    for order in range(1, degree_total - 1):
        series.append(
            ((2 * order + 1) * coord * series[order] - order * series[order - 1]) / (order + 1)
        )
    return series


def exact_dot(left, right):
    return jnp.dot(left, right, precision=highest, preferred_element_type=jnp.float32)


def transposed_dot(left, right):
    return lax.dot_general(
        left, right, (((1,), (1,)), ((), ())), precision=highest, preferred_element_type=jnp.float32
    )


def split_bf16(value):
    high = value.astype(jnp.bfloat16)
    low = (value - high.astype(jnp.float32)).astype(jnp.bfloat16)
    return high, low


def iota(shape, axis):
    return lax.broadcasted_iota(jnp.int32, shape, axis)


def build_features(ids_ref, positions_ref, throughput_ref, flags_ref):
    exposures, fibers = throughput_ref.shape
    rows = exposures * fibers
    total = positions_ref.shape[1]
    pick = (iota((total, fibers), 0) == ids_ref[...]).astype(jnp.float32)
    coords = exact_dot(positions_ref[...], pick)
    column = iota((fibers, rows), 1)
    spread = functools.reduce(
        jnp.logical_or,
        [iota((fibers, rows), 0) + e * fibers == column for e in range(exposures)],
    ).astype(jnp.float32)
    at = iota((exposures, rows), 1) - iota((exposures, rows), 0) * fibers
    own = (at >= 0) & (at < fibers)

    def widen(value):
        return jnp.sum(jnp.where(own, exact_dot(value, spread), 0.0), axis=0, keepdims=True)

    coords = exact_dot(coords, spread)
    coord_x, coord_y = coords[0:1], coords[1:2]
    through = widen(throughput_ref[...])
    flags = widen(flags_ref[...].astype(jnp.float32))
    series_x = legendre_series(coord_x, moment_degrees)
    series_y = legendre_series(coord_y, moment_degrees)
    sub = iota((padded_degrees, rows), 0)
    stack_y = jnp.zeros((padded_degrees, rows), jnp.float32)
    for order in range(moment_degrees):
        stack_y = jnp.where(sub == order, series_y[order], stack_y)
    scale = through * through * flags
    moments = jnp.concatenate([stack_y * (one * scale) for one in series_x], axis=0)
    poly_x, poly_y = legendre(coord_x), legendre(coord_y)
    sub = iota((PARAMS, rows), 0)
    design = jnp.zeros((PARAMS, rows), jnp.float32)
    for k in range(PARAMS):
        value = poly_x[k // basis_degrees] * poly_y[k % basis_degrees]
        design = jnp.where(sub == k, value * through, design)
    return moments, design * flags, design


def solve_block(table, moments, right):
    width = right.shape[1]
    normal = exact_dot(table, moments)
    sub = iota((PARAMS, width), 0)
    cols = [
        normal[k * PARAMS:(k + 1) * PARAMS] + jnp.where(sub == k, prior_weight, 0.0)
        for k in range(PARAMS)
    ]
    factor, inverse, interim = [], [], []
    for k in range(PARAMS):
        pivot = cols[k][k:k + 1]
        root = lax.rsqrt(pivot)
        root = root * (1.5 - 0.5 * pivot * root * root)
        inverse.append(root)
        line = cols[k] * root
        factor.append(line)
        value = right[k:k + 1] * root
        interim.append(value)
        right = right - line * value
        for j in range(k + 1, PARAMS):
            cols[j] = cols[j] - line * line[j:j + 1]
    solved = jnp.zeros((PARAMS, width), jnp.float32)
    for k in reversed(range(PARAMS)):
        known = jnp.sum(jnp.where(sub > k, factor[k] * solved, 0.0), axis=0, keepdims=True)
        solved = jnp.where(sub == k, (interim[k] - known) * inverse[k], solved)
    return solved


def kernel(
    fiber_size, wave_size, slices,
    ids_hbm, positions_hbm, throughput_hbm, flags_hbm, table_hbm,
    spectra_hbm, ivar_hbm, bits_hbm,
    residual_ref, chi_ref, coeffs_ref,
    ids_ref, positions_ref, throughput_ref, flags_ref, table_ref,
    flux, noise, bits, moments, gather1, partial, gather2,
    rights, right_gather1, right_partial, right_gather2, coeffs,
    chi_mine, chi_other,
    small_sem, load_sem, send_sem, recv_sem, chi_sem,
):
    exposures, fibers, waves = flux.shape
    rows = exposures * fibers
    high_size = fiber_size // low_size
    block = waves // (slices * fiber_size)
    chunk = high_size * block
    me = lax.axis_index("fiber")
    wave_me = lax.axis_index("wave")
    low, high = lax.rem(me, low_size), me // low_size
    low_peer = [high * low_size + lax.rem(low + d, low_size) for d in range(low_size)]
    high_peer = [lax.rem(high + d, high_size) * low_size + low for d in range(high_size)]

    barrier = pltpu.get_barrier_semaphore()
    for peer in low_peer[1:] + high_peer[1:]:
        pl.semaphore_signal(barrier, inc=1, device_id={"fiber": peer}, device_id_type=MESH)
    pl.semaphore_signal(barrier, inc=1, device_id={"wave": 1 - wave_me}, device_id_type=MESH)

    order = [(s, d) for s in range(slices) for d in list(range(1, low_size)) + [0]]

    def span(s, d):
        group = lax.rem(low + d, low_size)
        return group, pl.ds(pl.multiple_of(s * low_size * chunk + group * chunk, chunk), chunk)

    small = []
    for n, (source, target) in enumerate((
        (ids_hbm, ids_ref), (positions_hbm, positions_ref), (throughput_hbm, throughput_ref),
        (flags_hbm, flags_ref), (table_hbm, table_ref),
    )):
        copy = pltpu.make_async_copy(source, target, small_sem.at[n])
        copy.start()
        small.append(copy)
    loads = []
    for at, (s, d) in enumerate(order):
        where = span(s, d)[1]
        copies = []
        for n, (source, target) in enumerate(
            ((spectra_hbm, flux), (ivar_hbm, noise), (bits_hbm, bits))
        ):
            copy = pltpu.make_async_copy(
                source.at[:, :, where], target.at[:, :, where], load_sem.at[at, n]
            )
            copy.start()
            copies.append(copy)
        loads.append(copies)

    for copy in small:
        copy.wait()
    feature, right_feature, design = build_features(
        ids_ref, positions_ref, throughput_ref, flags_ref
    )
    eye = (iota((rows, rows), 0) == iota((rows, rows), 1)).astype(jnp.float32)
    design_high, design_low = split_bf16(transposed_dot(eye, design))
    design_wide = jnp.concatenate([design_high, design_low, design_high], axis=1)

    pl.semaphore_wait(barrier, low_size - 1 + high_size - 1 + 1)

    def remote(stage, s, d, source, target, peer):
        return pltpu.make_async_remote_copy(
            src_ref=source, dst_ref=target,
            send_sem=send_sem.at[s, stage, d - 1], recv_sem=recv_sem.at[s, stage, d - 1],
            device_id={"fiber": peer}, device_id_type=MESH,
        )

    started = []
    first, right_first = {}, {}
    for at, (s, d) in enumerate(order):
        group, where = span(s, d)
        for copy in loads[at]:
            copy.wait()
        good = (bits[:, :, where] & bad_bits) == 0
        weight = jnp.where(good, noise[:, :, where], 0.0)
        noise[:, :, where] = weight
        scaled = (weight * flux[:, :, where]).reshape(rows, chunk)
        normal = exact_dot(feature, weight.reshape(rows, chunk))
        right = exact_dot(right_feature, scaled)
        for b in range(high_size):
            lane = slice(b * block, (b + 1) * block)
            moments[s, group, b] = normal[:, lane]
            rights[s, b, group] = right[:, lane]
        if d:
            copy = remote(0, s, d, moments.at[s, group], gather1.at[s, d - 1], low_peer[d])
            copy.start()
            started.append(copy)
            first[s, d] = copy
        else:
            for e in range(1, high_size):
                to = lax.rem(high + e, high_size)
                copy = remote(
                    4, s, e, rights.at[s, to], right_gather1.at[s, e - 1], high_peer[e]
                )
                copy.start()
                started.append(copy)
                right_first[s, e] = copy

    def reduce_first(s):
        copies = []
        for e in range(1, high_size):
            right_first[s, e].wait_recv()
        for d in list(range(1, low_size)) + [0]:
            to = lax.rem(low + d, low_size)
            total = rights[s, high, to]
            for e in range(high_size - 1):
                total = total + right_gather1[s, e, to]
            right_partial[s, to] = total
            if d:
                copy = remote(
                    5, s, d, right_partial.at[s, to], right_gather2.at[s, d - 1], low_peer[d]
                )
                copy.start()
                copies.append(copy)
        for d in range(1, low_size):
            first[s, d].wait_recv()
        for d in list(range(1, high_size)) + [0]:
            to = lax.rem(high + d, high_size)
            total = moments[s, low, to]
            for e in range(low_size - 1):
                total = total + gather1[s, e, to]
            partial[s, to] = total
            if d:
                copy = remote(1, s, d, partial.at[s, to], gather2.at[s, d - 1], high_peer[d])
                copy.start()
                copies.append(copy)
        started.extend(copies)
        return copies

    def reduce_second(s, copies):
        for copy in copies:
            copy.wait_recv()
        total = partial[s, high]
        for e in range(high_size - 1):
            total = total + gather2[s, e]
        right = right_partial[s, low]
        for e in range(low_size - 1):
            right = right + right_gather2[s, e]
        solved = solve_block(table_ref[...], total, right)
        mine = coeffs.at[s, low * high_size + high]
        mine[...] = solved
        copies = []
        for d in range(1, high_size):
            copy = remote(2, s, d, mine, mine, high_peer[d])
            copy.start()
            copies.append(copy)
        started.extend(copies)
        return copies

    def spread_low(s, copies):
        for copy in copies:
            copy.wait_recv()
        mine = coeffs.at[s, pl.ds(low * high_size, high_size)]
        copies = []
        for d in range(1, low_size):
            copy = remote(3, s, d, mine, mine, low_peer[d])
            copy.start()
            copies.append(copy)
        started.extend(copies)
        return copies

    chi_total = [jnp.zeros((rows, lanes), jnp.float32)]

    def finish(s, copies):
        for copy in copies:
            copy.wait_recv()
        for group in range(low_size):
            start = (s * low_size + group) * chunk
            where = pl.ds(start, chunk)
            values = jnp.concatenate(
                [coeffs[s, group * high_size + b] for b in range(high_size)], axis=1
            )
            coeffs_ref[:, where] = values
            value_high, value_low = split_bf16(values)
            model = jnp.dot(
                design_wide,
                jnp.concatenate([value_high, value_high, value_low], axis=0),
                preferred_element_type=jnp.float32,
            )
            left = flux[:, :, where].reshape(rows, chunk) - model
            residual_ref[:, :, where] = left.reshape(exposures, fibers, chunk)
            term = noise[:, :, where].reshape(rows, chunk) * left * left
            for n in range(chunk // lanes):
                chi_total[0] = chi_total[0] + term[:, n * lanes:(n + 1) * lanes]

    stage = {}
    stage[0] = reduce_second(0, reduce_first(0))
    for s in range(1, slices):
        following = reduce_first(s)
        stage[s - 1] = spread_low(s - 1, stage[s - 1])
        stage[s] = reduce_second(s, following)
        finish(s - 1, stage[s - 1])
    finish(slices - 1, spread_low(slices - 1, stage[slices - 1]))

    chi_mine[...] = jnp.zeros_like(chi_mine)
    ones = jnp.ones((8, lanes), jnp.float32)
    for e in range(exposures):
        line = transposed_dot(ones, chi_total[0][e * fibers:(e + 1) * fibers])
        chi_mine[e:e + 1, :fibers] = line[0:1]
    copy = pltpu.make_async_remote_copy(
        src_ref=chi_mine, dst_ref=chi_other, send_sem=chi_sem.at[0], recv_sem=chi_sem.at[1],
        device_id={"wave": 1 - wave_me}, device_id_type=MESH,
    )
    copy.start()
    copy.wait()
    both = chi_mine[:exposures, :fibers] + chi_other[:exposures, :fibers]
    chi_ref[...] = both / (waves * wave_size)
    for copy in started:
        copy.wait_send()


def fused_body(fiber_size, wave_size, slices, spectra, inverse_var, mask_bits, sky_flags,
               fiber_ids, positions, throughput):
    exposures, fibers, waves = spectra.shape
    high_size = fiber_size // low_size
    block = waves // (slices * fiber_size)
    table = rebuild_table(padded_degrees)
    vmem = pl.BlockSpec(memory_space=pltpu.VMEM)
    cube = (exposures, fibers, waves)
    residual, chi, coeffs = pl.pallas_call(
        functools.partial(kernel, fiber_size, wave_size, slices),
        out_shape=(
            jax.ShapeDtypeStruct(cube, jnp.float32),
            jax.ShapeDtypeStruct((exposures, fibers), jnp.float32),
            jax.ShapeDtypeStruct((PARAMS, waves), jnp.float32),
        ),
        in_specs=[pl.BlockSpec(memory_space=pltpu.HBM)] * 8,
        out_specs=(vmem, vmem, vmem),
        scratch_shapes=[
            pltpu.VMEM((1, fibers), jnp.int32),
            pltpu.VMEM(positions.shape, jnp.float32),
            pltpu.VMEM((exposures, fibers), jnp.float32),
            pltpu.VMEM((exposures, fibers), jnp.int32),
            pltpu.VMEM(table.shape, jnp.float32),
            pltpu.VMEM(cube, jnp.float32),
            pltpu.VMEM(cube, jnp.float32),
            pltpu.VMEM(cube, jnp.int32),
            pltpu.VMEM((slices, low_size, high_size, moment_rows, block), jnp.float32),
            pltpu.VMEM((slices, low_size - 1, high_size, moment_rows, block), jnp.float32),
            pltpu.VMEM((slices, high_size, moment_rows, block), jnp.float32),
            pltpu.VMEM((slices, high_size - 1, moment_rows, block), jnp.float32),
            pltpu.VMEM((slices, high_size, low_size, PARAMS, block), jnp.float32),
            pltpu.VMEM((slices, high_size - 1, low_size, PARAMS, block), jnp.float32),
            pltpu.VMEM((slices, low_size, PARAMS, block), jnp.float32),
            pltpu.VMEM((slices, low_size - 1, PARAMS, block), jnp.float32),
            pltpu.VMEM((slices, fiber_size, PARAMS, block), jnp.float32),
            pltpu.VMEM((8, lanes), jnp.float32),
            pltpu.VMEM((8, lanes), jnp.float32),
            pltpu.SemaphoreType.DMA((5,)),
            pltpu.SemaphoreType.DMA((slices * low_size, 3)),
            pltpu.SemaphoreType.DMA((slices, 6, max(low_size, high_size) - 1)),
            pltpu.SemaphoreType.DMA((slices, 6, max(low_size, high_size) - 1)),
            pltpu.SemaphoreType.DMA((2,)),
        ],
        compiler_params=pltpu.CompilerParams(
            collective_id=0, has_side_effects=True, vmem_limit_bytes=40 * 1024 * 1024
        ),
    )(*[
        pltpu.with_memory_space_constraint(value, pltpu.HBM)
        for value in (fiber_ids.reshape(1, fibers), positions, throughput, sky_flags, table,
                      spectra, inverse_var, mask_bits)
    ])
    return residual, chi, coeffs


def solve_normal(matrix, right_side):
    param_count = right_side.shape[0]
    factor = {}
    for column in range(param_count):
        pivot_sum = matrix[column * param_count + column] + prior_weight
        for inner_k in range(column):
            pivot_sum = pivot_sum - factor[column, inner_k] * factor[column, inner_k]
        root_value = jnp.sqrt(pivot_sum)
        factor[column, column] = root_value
        for target in range(column + 1, param_count):
            running = matrix[target * param_count + column]
            for inner_k in range(column):
                running = running - factor[target, inner_k] * factor[column, inner_k]
            factor[target, column] = running / root_value
    interim = []
    for target in range(param_count):
        running = right_side[target]
        for inner_k in range(target):
            running = running - factor[target, inner_k] * interim[inner_k]
        interim.append(running / factor[target, target])
    solved = [None] * param_count
    for target in reversed(range(param_count)):
        running = interim[target]
        for inner_k in range(target + 1, param_count):
            running = running - factor[inner_k, target] * solved[inner_k]
        solved[target] = running / factor[target, target]
    return jnp.stack(solved)


def plain_body(spectra, inverse_var, mask_bits, sky_flags, fiber_ids, positions, throughput):
    exposures, fiber_count, wave_count = spectra.shape
    row_count = exposures * fiber_count
    coord_x = positions[0][fiber_ids]
    coord_y = positions[1][fiber_ids]

    def stack(first, second, scale):
        basis = jnp.stack([x * y for x in first for y in second], axis=-1)
        return (scale[:, :, None] * basis[None]).reshape(row_count, -1)

    design = stack(legendre(coord_x), legendre(coord_y), throughput)
    products = stack(
        legendre_series(coord_x, moment_degrees),
        legendre_series(coord_y, moment_degrees),
        throughput * throughput,
    )
    flux_rows = spectra.reshape(row_count, wave_count)
    usable = (mask_bits.reshape(row_count, wave_count) & bad_bits == 0).astype(jnp.float32)
    noise_weight = inverse_var.reshape(row_count, wave_count) * usable
    fit_weights = noise_weight * sky_flags.reshape(row_count).astype(jnp.float32)[:, None]
    normal = jnp.dot(products.T, fit_weights, precision=highest)
    right_side = jnp.dot(design.T, fit_weights * flux_rows, precision=highest)
    normal, right_side = lax.psum((normal, right_side), "fiber")
    normal = jnp.dot(rebuild_table(moment_degrees), normal, precision=highest)
    sky_coeffs = solve_normal(normal, right_side)
    residual = flux_rows - jnp.dot(design, sky_coeffs, precision=highest)
    chi_local = jnp.sum(noise_weight * residual * residual, axis=1)
    chi_total = lax.psum(chi_local, "wave")
    chi_square = (chi_total / (wave_count * lax.axis_size("wave"))).reshape(exposures, fiber_count)
    return (residual.reshape(exposures, fiber_count, wave_count), chi_square, sky_coeffs)


def choose_body(fiber_size, wave_size, spectra, *rest):
    exposures, fibers, waves = spectra.shape
    whole = fiber_size % low_size == 0 and fiber_size > low_size and wave_size == 2
    if whole and fibers % 8 == 0 and fibers <= lanes and exposures <= 8:
        for slices in (2, 1):
            if waves % (slices * fiber_size * lanes) == 0:
                return fused_body(fiber_size, wave_size, slices, spectra, *rest)
    return plain_body(spectra, *rest)


def solution(mesh):
    placed = (
        P(None, "fiber", "wave"),
        P(None, "fiber", "wave"),
        P(None, "fiber", "wave"),
        P(None, "fiber"),
        P("fiber"),
        P(),
        P(None, "fiber"),
    )
    return jax.shard_map(
        functools.partial(choose_body, mesh.shape["fiber"], mesh.shape["wave"]),
        mesh=mesh,
        in_specs=placed,
        out_specs=(P(None, "fiber", "wave"), P(None, "fiber"), P(None, "wave")),
        check_vma=False,
    )
```

```python
import functools

import jax
import jax.numpy as jnp
from jax import lax
from jax.experimental import pallas as pl
from jax.experimental.pallas import tpu as pltpu
from jax.sharding import PartitionSpec as P

PARAMS = 16

bad_bits = 31
prior_weight = 1.0
highest = lax.Precision.HIGHEST
moment_degrees = 7
basis_degrees = 4
moment_rows = moment_degrees * moment_degrees
lead_rows = moment_rows // 8 * 8
sent_rows = lead_rows + 8
lanes = 128
low_size = 4
MESH = pl.DeviceIdType.MESH


def monomial_table(degree_total):
    coeffs = [[0.0] * degree_total for order in range(degree_total)]
    coeffs[0][0] = 1.0
    coeffs[1][1] = 1.0
    for order in range(1, degree_total - 1):
        for power in range(degree_total):
            raised = coeffs[order][power - 1] if power >= 1 else 0.0
            coeffs[order + 1][power] = (
                (2 * order + 1) * raised - order * coeffs[order - 1][power]
            ) / (order + 1)
    return coeffs


def product_series(higher, first, second):
    product = [0.0] * moment_degrees
    for left_power in range(moment_degrees):
        for right_power in range(moment_degrees - left_power):
            product[left_power + right_power] += (
                higher[first][left_power] * higher[second][right_power]
            )
    series = [0.0] * moment_degrees
    for order in reversed(range(moment_degrees)):
        weight_now = product[order] / higher[order][order]
        series[order] = weight_now
        for power in range(moment_degrees):
            product[power] -= weight_now * higher[order][power]
    return series


def rebuild_table(row_degrees):
    higher = monomial_table(moment_degrees)
    pair = [
        [product_series(higher, first, second) for second in range(basis_degrees)]
        for first in range(basis_degrees)
    ]
    degrees = range(basis_degrees)
    return jnp.asarray(
        [
            [
                pair[i][k][a] * pair[j][l][b] if b < moment_degrees else 0.0
                for a in range(moment_degrees)
                for b in range(row_degrees)
            ]
            for i in degrees
            for j in degrees
            for k in degrees
            for l in degrees
        ],
        jnp.float32,
    )


def legendre(coord):
    return [
        jnp.ones_like(coord),
        coord,
        1.5 * coord * coord - 0.5,
        (2.5 * coord * coord - 1.5) * coord,
    ]


def legendre_series(coord, degree_total):
    series = [jnp.ones_like(coord), coord]
    for order in range(1, degree_total - 1):
        series.append(
            ((2 * order + 1) * coord * series[order] - order * series[order - 1]) / (order + 1)
        )
    return series


def exact_dot(left, right):
    return jnp.dot(left, right, precision=highest, preferred_element_type=jnp.float32)


def transposed_dot(left, right):
    return lax.dot_general(
        left, right, (((1,), (1,)), ((), ())), precision=highest, preferred_element_type=jnp.float32
    )


def split_bf16(value):
    high = value.astype(jnp.bfloat16)
    low = (value - high.astype(jnp.float32)).astype(jnp.bfloat16)
    return high, low


def iota(shape, axis):
    return lax.broadcasted_iota(jnp.int32, shape, axis)


def build_features(ids_ref, positions_ref, throughput_ref, flags_ref):
    exposures, fibers = throughput_ref.shape
    rows = exposures * fibers
    total = positions_ref.shape[1]
    pick = (iota((total, fibers), 0) == ids_ref[...]).astype(jnp.float32)
    coords = exact_dot(positions_ref[...], pick)
    column = iota((fibers, rows), 1)
    spread = functools.reduce(
        jnp.logical_or,
        [iota((fibers, rows), 0) + e * fibers == column for e in range(exposures)],
    ).astype(jnp.float32)
    at = iota((exposures, rows), 1) - iota((exposures, rows), 0) * fibers
    own = (at >= 0) & (at < fibers)

    def widen(value):
        return jnp.sum(jnp.where(own, exact_dot(value, spread), 0.0), axis=0, keepdims=True)

    coords = exact_dot(coords, spread)
    coord_x, coord_y = coords[0:1], coords[1:2]
    through = widen(throughput_ref[...])
    flags = widen(flags_ref[...].astype(jnp.float32))
    series_x = legendre_series(coord_x, moment_degrees)
    series_y = legendre_series(coord_y, moment_degrees)
    scale = through * through * flags
    sub = iota((moment_rows, rows), 0)
    moments = jnp.zeros((moment_rows, rows), jnp.float32)
    spread_y = jnp.zeros((moment_rows, rows), jnp.float32)
    for order in range(moment_degrees):
        first_row = order * moment_degrees
        in_x = (sub >= first_row) & (sub < first_row + moment_degrees)
        moments = jnp.where(in_x, series_x[order] * scale, moments)
        in_y = functools.reduce(
            jnp.logical_or, [sub == a * moment_degrees + order for a in range(moment_degrees)]
        )
        spread_y = jnp.where(in_y, series_y[order], spread_y)
    moments = moments * spread_y
    poly_x, poly_y = legendre(coord_x), legendre(coord_y)
    sub = iota((PARAMS, rows), 0)
    design = jnp.zeros((PARAMS, rows), jnp.float32)
    for k in range(PARAMS):
        value = poly_x[k // basis_degrees] * poly_y[k % basis_degrees]
        design = jnp.where(sub == k, value * through, design)
    return moments, design * flags, design


def solve_block(table, moments, right):
    width = right.shape[1]
    normal = exact_dot(table, moments[:moment_rows])
    sub = iota((PARAMS, width), 0)
    cols = [
        normal[k * PARAMS:(k + 1) * PARAMS] + jnp.where(sub == k, prior_weight, 0.0)
        for k in range(PARAMS)
    ]
    factor, inverse, interim = [], [], []
    for k in range(PARAMS):
        pivot = cols[k][k:k + 1]
        root = lax.rsqrt(pivot)
        root = root * (1.5 - 0.5 * pivot * root * root)
        inverse.append(root)
        line = cols[k] * root
        factor.append(line)
        value = right[k:k + 1] * root
        interim.append(value)
        right = right - line * value
        for j in range(k + 1, PARAMS):
            cols[j] = cols[j] - line * line[j:j + 1]
    solved = jnp.zeros((PARAMS, width), jnp.float32)
    for k in reversed(range(PARAMS)):
        known = jnp.sum(jnp.where(sub > k, factor[k] * solved, 0.0), axis=0, keepdims=True)
        solved = jnp.where(sub == k, (interim[k] - known) * inverse[k], solved)
    return solved


def kernel(
    fiber_size, wave_size, slices,
    ids_hbm, positions_hbm, throughput_hbm, flags_hbm, table_hbm,
    spectra_hbm, ivar_hbm, bits_hbm,
    residual_ref, chi_ref, coeffs_ref,
    ids_ref, positions_ref, throughput_ref, flags_ref, table_ref,
    flux, noise, bits, moments, gather1, partial, gather2,
    rights, right_gather1, right_partial, right_gather2, coeffs,
    chi_mine, chi_other,
    small_sem, load_sem, send_sem, recv_sem, chi_sem,
):
    exposures, fibers, waves = flux.shape
    rows = exposures * fibers
    high_size = fiber_size // low_size
    block = waves // (slices * fiber_size)
    chunk = high_size * block
    me = lax.axis_index("fiber")
    wave_me = lax.axis_index("wave")
    low, high = lax.rem(me, low_size), me // low_size
    low_peer = [high * low_size + lax.rem(low + d, low_size) for d in range(low_size)]
    high_peer = [lax.rem(high + d, high_size) * low_size + low for d in range(high_size)]

    barrier = pltpu.get_barrier_semaphore()
    for peer in low_peer[1:] + high_peer[1:]:
        pl.semaphore_signal(barrier, inc=1, device_id={"fiber": peer}, device_id_type=MESH)
    pl.semaphore_signal(barrier, inc=1, device_id={"wave": 1 - wave_me}, device_id_type=MESH)

    order = [(s, d) for s in range(slices) for d in list(range(1, low_size)) + [0]]

    def span(s, d):
        group = lax.rem(low + d, low_size)
        return group, pl.ds(pl.multiple_of(s * low_size * chunk + group * chunk, chunk), chunk)

    small = []
    for n, (source, target) in enumerate((
        (ids_hbm, ids_ref), (positions_hbm, positions_ref), (throughput_hbm, throughput_ref),
        (flags_hbm, flags_ref), (table_hbm, table_ref),
    )):
        copy = pltpu.make_async_copy(source, target, small_sem.at[n])
        copy.start()
        small.append(copy)
    loads = []
    for at, (s, d) in enumerate(order):
        where = span(s, d)[1]
        copies = []
        for n, (source, target) in enumerate(
            ((spectra_hbm, flux), (ivar_hbm, noise), (bits_hbm, bits))
        ):
            copy = pltpu.make_async_copy(
                source.at[:, :, where], target.at[:, :, where], load_sem.at[at, n]
            )
            copy.start()
            copies.append(copy)
        loads.append(copies)

    for copy in small:
        copy.wait()
    feature, right_feature, design = build_features(
        ids_ref, positions_ref, throughput_ref, flags_ref
    )
    eye = (iota((rows, rows), 0) == iota((rows, rows), 1)).astype(jnp.float32)
    design_high, design_low = split_bf16(transposed_dot(eye, design))
    design_wide = jnp.concatenate([design_high, design_low, design_high], axis=1)

    pl.semaphore_wait(barrier, low_size - 1 + high_size - 1 + 1)

    def remote(stage, s, d, source, target, peer):
        return pltpu.make_async_remote_copy(
            src_ref=source, dst_ref=target,
            send_sem=send_sem.at[s, stage, d - 1], recv_sem=recv_sem.at[s, stage, d - 1],
            device_id={"fiber": peer}, device_id_type=MESH,
        )

    tail_row = high_size * lead_rows
    started = []
    first, right_first = {}, {}
    for at, (s, d) in enumerate(order):
        group, where = span(s, d)
        for copy in loads[at]:
            copy.wait()
        good = (bits[:, :, where] & bad_bits) == 0
        weight = jnp.where(good, noise[:, :, where], 0.0)
        noise[:, :, where] = weight
        scaled = (weight * flux[:, :, where]).reshape(rows, chunk)
        normal = exact_dot(feature, weight.reshape(rows, chunk))
        right = exact_dot(right_feature, scaled)
        for b in range(high_size):
            lane = slice(b * block, (b + 1) * block)
            moments[s, group, b * lead_rows:(b + 1) * lead_rows] = normal[:lead_rows, lane]
            moments[s, group, tail_row + b:tail_row + b + 1] = normal[lead_rows:moment_rows, lane]
            rights[s, b, group] = right[:, lane]
        if d:
            copy = remote(0, s, d, moments.at[s, group], gather1.at[s, d - 1], low_peer[d])
            copy.start()
            started.append(copy)
            first[s, d] = copy
        else:
            for e in range(1, high_size):
                to = lax.rem(high + e, high_size)
                copy = remote(
                    4, s, e, rights.at[s, to], right_gather1.at[s, e - 1], high_peer[e]
                )
                copy.start()
                started.append(copy)
                right_first[s, e] = copy

    def reduce_first(s):
        copies = []
        for e in range(1, high_size):
            right_first[s, e].wait_recv()
        for d in list(range(1, low_size)) + [0]:
            to = lax.rem(low + d, low_size)
            total = rights[s, high, to]
            for e in range(high_size - 1):
                total = total + right_gather1[s, e, to]
            right_partial[s, to] = total
            if d:
                copy = remote(
                    5, s, d, right_partial.at[s, to], right_gather2.at[s, d - 1], low_peer[d]
                )
                copy.start()
                copies.append(copy)
        for d in range(1, low_size):
            first[s, d].wait_recv()
        for d in list(range(1, high_size)) + [0]:
            to = lax.rem(high + d, high_size)
            lead = pl.ds(pl.multiple_of(to * lead_rows, 8), lead_rows)
            tail = pl.ds(tail_row + to, 1)
            total, last = moments[s, low, lead], moments[s, low, tail]
            for e in range(low_size - 1):
                total = total + gather1[s, e, lead]
                last = last + gather1[s, e, tail]
            partial[s, to, :lead_rows] = total
            partial[s, to, lead_rows:] = jnp.broadcast_to(last, (8, block))
            if d:
                copy = remote(1, s, d, partial.at[s, to], gather2.at[s, d - 1], high_peer[d])
                copy.start()
                copies.append(copy)
        started.extend(copies)
        return copies

    def reduce_second(s, copies):
        for copy in copies:
            copy.wait_recv()
        total = partial[s, high]
        for e in range(high_size - 1):
            total = total + gather2[s, e]
        right = right_partial[s, low]
        for e in range(low_size - 1):
            right = right + right_gather2[s, e]
        solved = solve_block(table_ref[...], total, right)
        mine = coeffs.at[s, low * high_size + high]
        mine[...] = solved
        copies = []
        for d in range(1, high_size):
            copy = remote(2, s, d, mine, mine, high_peer[d])
            copy.start()
            copies.append(copy)
        started.extend(copies)
        return copies

    def spread_low(s, copies):
        for copy in copies:
            copy.wait_recv()
        mine = coeffs.at[s, pl.ds(low * high_size, high_size)]
        copies = []
        for d in range(1, low_size):
            copy = remote(3, s, d, mine, mine, low_peer[d])
            copy.start()
            copies.append(copy)
        started.extend(copies)
        return copies

    chi_total = [jnp.zeros((rows, lanes), jnp.float32)]

    def finish(s, copies):
        for d in range(low_size):
            if d:
                copies[d - 1].wait_recv()
            group, where = span(s, low_size - d)
            values = jnp.concatenate(
                [coeffs[s, group * high_size + b] for b in range(high_size)], axis=1
            )
            coeffs_ref[:, where] = values
            value_high, value_low = split_bf16(values)
            model = jnp.dot(
                design_wide,
                jnp.concatenate([value_high, value_high, value_low], axis=0),
                preferred_element_type=jnp.float32,
            )
            left = flux[:, :, where].reshape(rows, chunk) - model
            residual_ref[:, :, where] = left.reshape(exposures, fibers, chunk)
            term = noise[:, :, where].reshape(rows, chunk) * left * left
            for n in range(chunk // lanes):
                chi_total[0] = chi_total[0] + term[:, n * lanes:(n + 1) * lanes]

    stage = {}
    stage[0] = reduce_second(0, reduce_first(0))
    for s in range(1, slices):
        following = reduce_first(s)
        stage[s - 1] = spread_low(s - 1, stage[s - 1])
        stage[s] = reduce_second(s, following)
        finish(s - 1, stage[s - 1])
    finish(slices - 1, spread_low(slices - 1, stage[slices - 1]))

    chi_mine[...] = jnp.zeros_like(chi_mine)
    ones = jnp.ones((8, lanes), jnp.float32)
    for e in range(exposures):
        line = transposed_dot(ones, chi_total[0][e * fibers:(e + 1) * fibers])
        chi_mine[e:e + 1, :fibers] = line[0:1]
    copy = pltpu.make_async_remote_copy(
        src_ref=chi_mine, dst_ref=chi_other, send_sem=chi_sem.at[0], recv_sem=chi_sem.at[1],
        device_id={"wave": 1 - wave_me}, device_id_type=MESH,
    )
    copy.start()
    copy.wait()
    both = chi_mine[:exposures, :fibers] + chi_other[:exposures, :fibers]
    chi_ref[...] = both / (waves * wave_size)
    for copy in started:
        copy.wait_send()


def fused_body(fiber_size, wave_size, slices, spectra, inverse_var, mask_bits, sky_flags,
               fiber_ids, positions, throughput):
    exposures, fibers, waves = spectra.shape
    high_size = fiber_size // low_size
    block = waves // (slices * fiber_size)
    table = rebuild_table(moment_degrees)
    group_rows = high_size * lead_rows + -(-high_size // 8) * 8
    vmem = pl.BlockSpec(memory_space=pltpu.VMEM)
    cube = (exposures, fibers, waves)
    residual, chi, coeffs = pl.pallas_call(
        functools.partial(kernel, fiber_size, wave_size, slices),
        out_shape=(
            jax.ShapeDtypeStruct(cube, jnp.float32),
            jax.ShapeDtypeStruct((exposures, fibers), jnp.float32),
            jax.ShapeDtypeStruct((PARAMS, waves), jnp.float32),
        ),
        in_specs=[pl.BlockSpec(memory_space=pltpu.HBM)] * 8,
        out_specs=(vmem, vmem, vmem),
        scratch_shapes=[
            pltpu.VMEM((1, fibers), jnp.int32),
            pltpu.VMEM(positions.shape, jnp.float32),
            pltpu.VMEM((exposures, fibers), jnp.float32),
            pltpu.VMEM((exposures, fibers), jnp.int32),
            pltpu.VMEM(table.shape, jnp.float32),
            pltpu.VMEM(cube, jnp.float32),
            pltpu.VMEM(cube, jnp.float32),
            pltpu.VMEM(cube, jnp.int32),
            pltpu.VMEM((slices, low_size, group_rows, block), jnp.float32),
            pltpu.VMEM((slices, low_size - 1, group_rows, block), jnp.float32),
            pltpu.VMEM((slices, high_size, sent_rows, block), jnp.float32),
            pltpu.VMEM((slices, high_size - 1, sent_rows, block), jnp.float32),
            pltpu.VMEM((slices, high_size, low_size, PARAMS, block), jnp.float32),
            pltpu.VMEM((slices, high_size - 1, low_size, PARAMS, block), jnp.float32),
            pltpu.VMEM((slices, low_size, PARAMS, block), jnp.float32),
            pltpu.VMEM((slices, low_size - 1, PARAMS, block), jnp.float32),
            pltpu.VMEM((slices, fiber_size, PARAMS, block), jnp.float32),
            pltpu.VMEM((8, lanes), jnp.float32),
            pltpu.VMEM((8, lanes), jnp.float32),
            pltpu.SemaphoreType.DMA((5,)),
            pltpu.SemaphoreType.DMA((slices * low_size, 3)),
            pltpu.SemaphoreType.DMA((slices, 6, max(low_size, high_size) - 1)),
            pltpu.SemaphoreType.DMA((slices, 6, max(low_size, high_size) - 1)),
            pltpu.SemaphoreType.DMA((2,)),
        ],
        compiler_params=pltpu.CompilerParams(
            collective_id=0, has_side_effects=True, vmem_limit_bytes=40 * 1024 * 1024
        ),
    )(*[
        pltpu.with_memory_space_constraint(value, pltpu.HBM)
        for value in (fiber_ids.reshape(1, fibers), positions, throughput, sky_flags, table,
                      spectra, inverse_var, mask_bits)
    ])
    return residual, chi, coeffs


def solve_normal(matrix, right_side):
    param_count = right_side.shape[0]
    factor = {}
    for column in range(param_count):
        pivot_sum = matrix[column * param_count + column] + prior_weight
        for inner_k in range(column):
            pivot_sum = pivot_sum - factor[column, inner_k] * factor[column, inner_k]
        root_value = jnp.sqrt(pivot_sum)
        factor[column, column] = root_value
        for target in range(column + 1, param_count):
            running = matrix[target * param_count + column]
            for inner_k in range(column):
                running = running - factor[target, inner_k] * factor[column, inner_k]
            factor[target, column] = running / root_value
    interim = []
    for target in range(param_count):
        running = right_side[target]
        for inner_k in range(target):
            running = running - factor[target, inner_k] * interim[inner_k]
        interim.append(running / factor[target, target])
    solved = [None] * param_count
    for target in reversed(range(param_count)):
        running = interim[target]
        for inner_k in range(target + 1, param_count):
            running = running - factor[inner_k, target] * solved[inner_k]
        solved[target] = running / factor[target, target]
    return jnp.stack(solved)


def plain_body(spectra, inverse_var, mask_bits, sky_flags, fiber_ids, positions, throughput):
    exposures, fiber_count, wave_count = spectra.shape
    row_count = exposures * fiber_count
    coord_x = positions[0][fiber_ids]
    coord_y = positions[1][fiber_ids]

    def stack(first, second, scale):
        basis = jnp.stack([x * y for x in first for y in second], axis=-1)
        return (scale[:, :, None] * basis[None]).reshape(row_count, -1)

    design = stack(legendre(coord_x), legendre(coord_y), throughput)
    products = stack(
        legendre_series(coord_x, moment_degrees),
        legendre_series(coord_y, moment_degrees),
        throughput * throughput,
    )
    flux_rows = spectra.reshape(row_count, wave_count)
    usable = (mask_bits.reshape(row_count, wave_count) & bad_bits == 0).astype(jnp.float32)
    noise_weight = inverse_var.reshape(row_count, wave_count) * usable
    fit_weights = noise_weight * sky_flags.reshape(row_count).astype(jnp.float32)[:, None]
    normal = jnp.dot(products.T, fit_weights, precision=highest)
    right_side = jnp.dot(design.T, fit_weights * flux_rows, precision=highest)
    normal, right_side = lax.psum((normal, right_side), "fiber")
    normal = jnp.dot(rebuild_table(moment_degrees), normal, precision=highest)
    sky_coeffs = solve_normal(normal, right_side)
    residual = flux_rows - jnp.dot(design, sky_coeffs, precision=highest)
    chi_local = jnp.sum(noise_weight * residual * residual, axis=1)
    chi_total = lax.psum(chi_local, "wave")
    chi_square = (chi_total / (wave_count * lax.axis_size("wave"))).reshape(exposures, fiber_count)
    return (residual.reshape(exposures, fiber_count, wave_count), chi_square, sky_coeffs)


def choose_body(fiber_size, wave_size, spectra, *rest):
    exposures, fibers, waves = spectra.shape
    whole = fiber_size % low_size == 0 and fiber_size > low_size and wave_size == 2
    if whole and fibers % 8 == 0 and fibers <= lanes and exposures <= 8:
        for slices in (2, 1):
            if waves % (slices * fiber_size * lanes) == 0:
                return fused_body(fiber_size, wave_size, slices, spectra, *rest)
    return plain_body(spectra, *rest)


def solution(mesh):
    placed = (
        P(None, "fiber", "wave"),
        P(None, "fiber", "wave"),
        P(None, "fiber", "wave"),
        P(None, "fiber"),
        P("fiber"),
        P(),
        P(None, "fiber"),
    )
    return jax.shard_map(
        functools.partial(choose_body, mesh.shape["fiber"], mesh.shape["wave"]),
        mesh=mesh,
        in_specs=placed,
        out_specs=(P(None, "fiber", "wave"), P(None, "fiber"), P(None, "wave")),
        check_vma=False,
    )
```
